256 devices in a mesh: tm: 8 (over z_hi, y), gy: 4 (over z_lo), gz: 8 (over x, core).
Axes of the slice: x: 4, y: 4, z: 8 (z_hi: 2, z_lo: 4; z = z_hi * 4 + z_lo), core: 2. Of those that a mesh axis runs over, the one named last changes fastest.
Arguments:
- inverse_mass: float32 [32, 128, 128], P('gy', 'gz'), may hold values from 0.5 to 2
- actuator_of_cell: int32 [32, 128, 128], P('gy', 'gz'), may hold values from 0 to 31
- plan_ids: int32 [8, 32], P('tm'), may hold values from 0 to 15
- profiles: float32 [16, 9], replicated, may hold values from -4 to 4
- directions: float32 [3, 32], replicated, may hold values from -4 to 4
Outputs:
- predicted_state: float32 [8, 6, 32, 128, 128], P('tm', None, 'gy', 'gz')
The draws below stay inside these ranges and needn't reach their ends.
All inputs are finite; a program needn't handle non-finite values.
Results may differ from the reference program's by a relative error of at most 0.00021.
Values sent between devices are 32-bit elements; how exact they have to be, the bound alone decides.
No kernel may reach another device: no remote copies, remote signals or barrier semaphores. Data moves between devices by JAX's collectives and lax.ppermute only.
A program may use at most 64 MiB of HBM per device.

```python
import math
import jax
import jax.numpy as jnp
import numpy as np

NX = 128
STEPS = 8
TERMS = 8
NACT = 32
NPROF = 16
WINDOWS = 8
NY = 32
NZ = 128


def with_ends(entries, key, smallest, top_value):
    extent = entries.shape
    spot = [jax.random.randint(jax.random.fold_in(key, axis), (), 0, extent[axis]) for axis in range(len(extent))]
    entries = entries.at[tuple(spot)].set(smallest)
    longest = extent.index(max(extent))
    spot[longest] = (spot[longest] + 1) % extent[longest]
    return entries.at[tuple(spot)].set(top_value)


def shard_levels(stream_key, dims, cuts, low, largest):
    def one(dim, shards_of):
        steps = jax.random.uniform(jax.random.fold_in(jax.random.fold_in(stream_key, 6), dim), (shards_of,), jnp.float32, low / len(cuts), largest / len(cuts))
        return jnp.repeat(jnp.exp(steps), dims[dim] // shards_of).reshape((-1,) + (1,) * (len(dims) - dim - 1))

    level = one(*cuts[0])
    for cut in cuts[1:]:
        level = level * one(*cut)
    return level


def centred(rng, extent, spread, limit, dtype=jnp.bfloat16):
    return jnp.clip(spread * jax.random.normal(rng, extent, jnp.float32), -limit, limit).astype(dtype)


def setup_inputs(seed: int = 0) -> dict:
    key_of = jax.random.split(jax.random.key(seed), 6)
    inverse_mass = jnp.clip(jnp.exp(math.log(2.0) - 1.3862944 * jax.random.uniform(key_of[0], (NY, NZ, NX), jnp.float32) ** shard_levels(key_of[0], (NY, NZ, NX), ((0, 4), (1, 8)), -0.2, 0.2)), 0.5, 2.0)
    actuator_of_cell = with_ends(jax.random.randint(key_of[1], (NY, NZ, NX), 0, NACT), jax.random.fold_in(key_of[1], 1), 0, NACT - 1).astype(jnp.int32)
    plan_ids = with_ends(jax.random.randint(key_of[2], (WINDOWS, NACT), 0, NPROF), jax.random.fold_in(key_of[2], 1), 0, NPROF - 1).astype(jnp.int32)
    profiles = centred(key_of[3], (NPROF, STEPS + 1), 1.0, 4.0, jnp.float32)
    directions = centred(key_of[4], (3, NACT), 1.0, 4.0, jnp.float32)
    return dict(inverse_mass=inverse_mass, actuator_of_cell=actuator_of_cell, plan_ids=plan_ids, profiles=profiles, directions=directions)


lame_ratio = 2.5
mass_top = 2.0
step_squared = 1.0

def cheb_tables():
    spectrum_top = mass_top * 12.0 * (1.0 + lame_ratio)
    time_step = math.sqrt(step_squared / spectrum_top)
    horizon = STEPS * time_step
    angles = np.pi * (np.arange(TERMS) + 0.5) / TERMS
    node_x = 0.5 * spectrum_top * (1.0 + np.cos(angles))
    node_root = np.sqrt(node_x)
    values_c = np.cos(horizon * node_root)
    values_s = np.sin(horizon * node_root) / node_root
    values_g = node_root * np.sin(horizon * node_root)

    def project_values(values):
        result = np.array([2.0 / TERMS * np.sum(values * np.cos(k * angles)) for k in range(TERMS)])
        result[0] = 0.5 * result[0]
        return [float(entry) for entry in result]
    return (spectrum_top, time_step, project_values(values_c), project_values(values_s), project_values(values_g))

def stiffness(padded, inverse_mass):
    size_y = padded.shape[-3] - 2
    size_z = padded.shape[-2] - 2
    size_x = padded.shape[-1] - 2
    centre = padded[..., 1:size_y + 1, 1:size_z + 1, 1:size_x + 1]
    beside = padded[..., 2:, 1:size_z + 1, 1:size_x + 1] + padded[..., :size_y, 1:size_z + 1, 1:size_x + 1]
    beside = beside + padded[..., 1:size_y + 1, 2:, 1:size_x + 1] + padded[..., 1:size_y + 1, :size_z, 1:size_x + 1]
    beside = beside + padded[..., 1:size_y + 1, 1:size_z + 1, 2:] + padded[..., 1:size_y + 1, 1:size_z + 1, :size_x]
    laplace_term = 6.0 * centre - beside
    lower = padded[..., :size_y + 1, :size_z + 1, :size_x + 1]
    divergence = padded[..., 0, 1:, :size_z + 1, :size_x + 1] - lower[..., 0, :, :, :]
    divergence = divergence + (padded[..., 1, :size_y + 1, 1:, :size_x + 1] - lower[..., 1, :, :, :])
    divergence = divergence + (padded[..., 2, :size_y + 1, :size_z + 1, 1:] - lower[..., 2, :, :, :])
    inner = divergence[..., 1:, 1:, 1:]
    gradient = jnp.stack([divergence[..., :size_y, 1:, 1:] - inner, divergence[..., 1:, :size_z, 1:] - inner, divergence[..., 1:, 1:, :size_x] - inner], axis=-4)
    return inverse_mass * (laplace_term + lame_ratio * gradient)

def pad_full(field):
    return jnp.pad(field, [(0, 0)] * (field.ndim - 3) + [(1, 1)] * 3)

def leapfrog(force, amplitude, apply_op):
    spectrum_top, time_step, coef_c, coef_s, coef_g = cheb_tables()
    half_step = 0.5 * time_step
    displace = jnp.zeros_like(force)
    velocity = jnp.zeros_like(force)
    stiff_term = jnp.zeros_like(force)
    for n in range(STEPS):
        half_velocity = velocity + half_step * (force * amplitude[n] - stiff_term)
        displace = displace + time_step * half_velocity
        stiff_term = apply_op(displace)
        velocity = half_velocity + half_step * (force * amplitude[n + 1] - stiff_term)
    return jnp.concatenate([displace, velocity], axis=0)

def propagate(state, apply_op):
    spectrum_top, time_step, coef_c, coef_s, coef_g = cheb_tables()
    scale = 2.0 / spectrum_top
    second_table = jnp.asarray([[coef_g[k], coef_s[k]] for k in range(TERMS)], jnp.float32).reshape(TERMS, 2, 1, 1, 1, 1)
    previous = state.reshape((2, 3) + state.shape[1:])
    first = coef_c[0] * previous
    second = second_table[0] * previous
    current = scale * apply_op(previous) - previous
    for k in range(1, TERMS):
        first = first + coef_c[k] * current
        second = second + second_table[k] * current
        if k < TERMS - 1:
            shifted = scale * apply_op(current) - current
            previous, current = (current, 2.0 * shifted - previous)
    new_displace = first[0] + second[1]
    new_velocity = first[1] - second[0]
    return jnp.concatenate([new_displace, new_velocity], axis=0)

def reference(inverse_mass, actuator_of_cell, plan_ids, profiles, directions):

    def apply_op(field):
        return stiffness(pad_full(field), inverse_mass)
    force = inverse_mass[None] * directions[:, actuator_of_cell]
    end_states = []
    moved_once = []
    moved_twice = []
    for w in range(WINDOWS):
        chosen = profiles[plan_ids[w]]
        amplitude = jnp.moveaxis(chosen[actuator_of_cell], -1, 0)
        end_state = leapfrog(force, amplitude, apply_op)
        moved = propagate(end_state, apply_op)
        end_states.append(end_state)
        moved_once.append(moved)
        moved_twice.append(propagate(moved, apply_op))
    outputs = []
    for w in range(WINDOWS):
        total = end_states[w]
        total = total + (moved_once[w - 1] if w >= 1 else jnp.zeros_like(total))
        total = total + (moved_twice[w - 2] if w >= 2 else jnp.zeros_like(total))
        outputs.append(total)
    return jnp.stack(outputs)
```

```python
import functools
import math

import jax
import jax.numpy as jnp
import numpy as np
from jax import lax
from jax.experimental import pallas as pl
from jax.experimental.pallas import tpu as pltpu
from jax.sharding import PartitionSpec as P

STEPS = 8
TERMS = 8
lame_ratio = 2.5
mass_top = 2.0
step_squared = 1.0

PLANES = 32
OWN_Y = 8
OWN_Z = 16
HALO = 24
ROWS = HALO + OWN_Z + HALO
PAD = 8
LANES = 128
CHUNK = 8
UNROLL = 2


def cheb_tables():
    spectrum_top = mass_top * 12.0 * (1.0 + lame_ratio)
    time_step = math.sqrt(step_squared / spectrum_top)
    horizon = STEPS * time_step
    angles = np.pi * (np.arange(TERMS) + 0.5) / TERMS
    node_x = 0.5 * spectrum_top * (1.0 + np.cos(angles))
    node_root = np.sqrt(node_x)
    values_c = np.cos(horizon * node_root)
    values_s = np.sin(horizon * node_root) / node_root
    values_g = node_root * np.sin(horizon * node_root)

    def project_values(values):
        result = np.array([2.0 / TERMS * np.sum(values * np.cos(k * angles)) for k in range(TERMS)])
        result[0] = 0.5 * result[0]
        return [float(entry) for entry in result]

    return (
        spectrum_top,
        time_step,
        project_values(values_c),
        project_values(values_s),
        project_values(values_g),
    )


def columns(reach):
    return (HALO - reach) // 8, -(-(HALO + OWN_Z + reach) // 8)


def span(reach):
    count = min(8, reach) + OWN_Y + min(16, reach)
    return count + count % UNROLL


def kernel(
    place_ref, table_ref, far_left, left, own, right, far_right, out_ref,
    mass, mass4, diag, diag_x, actor, dirs, disp, vel, spare_u, spare_v, total, div_u, div_v,
):
    spectrum_top, time_step, coef_c, coef_s, coef_g = cheb_tables()
    here = place_ref[0]
    home = here * OWN_Y
    lane = lax.broadcasted_iota(jnp.int32, (CHUNK, LANES), 1)
    not_first = lane != 0
    not_last = lane != LANES - 1
    six_x = jnp.where(lane == 0, 6.0 + lame_ratio, 6.0).astype(jnp.float32)
    zero = jnp.zeros((CHUNK, LANES), jnp.float32)

    def after(value):
        return jnp.where(not_last, pltpu.roll(value, LANES - 1, 1), 0.0)

    def before(value):
        return jnp.where(not_first, pltpu.roll(value, 1, 1), 0.0)

    def rows_of(column):
        return PAD + column * 8

    def lowest(reach):
        return jnp.clip(home - reach, 0, PLANES - span(reach)) + 1

    def zero_array(ref, lead):
        @pl.loop(0, ref.shape[-3])
        def _(plane):
            for c in lead:
                ref[c + (plane,)] = jnp.zeros(ref.shape[-2:], ref.dtype)

    three = [(0,), (1,), (2,)]
    for ref in (disp, vel, spare_u, spare_v):
        zero_array(ref, three)

    for ref in (mass, mass4, diag, diag_x, div_u, div_v):
        zero_array(ref, [()])

    for slot in range(4):
        first = lax.rem(here + 4 - slot, 4) * OWN_Y + 1

        @pl.loop(0, OWN_Y)
        def _(y):
            plane = first + y
            row = 0
            for piece in (far_left, left, own, right, far_right):
                for part in range(0, piece.shape[-2], 8):
                    at = pl.ds(PAD + row, 8)
                    weight = piece[slot, 0, y, part : part + 8, :] * (1.0 / spectrum_top)
                    index = piece[slot, 1, y, part : part + 8, :].astype(jnp.int32)
                    mass[plane, at, :] = weight
                    mass4[plane, at, :] = 4.0 * weight
                    diag[plane, at, :] = 24.0 * weight - 2.0
                    diag_x[plane, at, :] = 4.0 * six_x * weight - 2.0
                    actor[plane, at, :] = index
                    for c in range(3):
                        dirs[c, plane, at, :] = jnp.take_along_axis(
                            table_ref[27 + c], index, axis=1, mode="promise_in_bounds"
                        )
                    row += 8

    def divergence(field, plane, at, low):
        a0, a1, a2 = (field[c, plane, at, :] for c in range(3))
        nxt = after(a2)
        value = (field[0, plane + 1, at, :] - a0) + (field[1, plane, pl.ds(low + 1, CHUNK), :] - a1)
        return (value + (nxt - a2)) * lame_ratio, nxt

    def parts(field, div, plane, low):
        at = pl.ds(low, CHUNK)
        u0, u1, u2 = (field[c, plane, at, :] for c in range(3))
        up = [field[c, plane + 1, at, :] for c in range(3)]
        down = [field[c, plane - 1, at, :] for c in range(3)]
        ahead = [field[c, plane, pl.ds(low + 1, CHUNK), :] for c in range(3)]
        behind = [field[c, plane, pl.ds(low - 1, CHUNK), :] for c in range(3)]
        next2 = after(u2)
        here_p = ((up[0] - u0) + (ahead[1] - u1) + (next2 - u2)) * lame_ratio
        div[plane, at, :] = here_p
        side = [(up[c] + down[c]) + (ahead[c] + behind[c]) for c in range(3)]
        sum0 = side[0] + (after(u0) + before(u0)) + (here_p - div[plane - 1, at, :])
        sum1 = side[1] + (after(u1) + before(u1)) + (here_p - div[plane, pl.ds(low - 1, CHUNK), :])
        sum2 = side[2] + (next2 + here_p) - before(here_p - u2)
        return (u0, u1, u2), (sum0, sum1, sum2)

    def sweep(reach, fields, head, each):
        j0, j1 = columns(reach)
        j0p = j0 - 1 if (HALO - reach) % 8 == 0 else j0
        begin = lowest(reach)

        def edges(plane, cols):
            for low in range(rows_of(cols[0]), rows_of(cols[1]), CHUNK):
                at = pl.ds(low, CHUNK)
                for field, div in fields:
                    div[plane, at, :] = divergence(field, plane, at, low)[0]

        if head is not None:
            head(begin - 1)
            head(begin)
        edges(begin - 1, (j0, j1))

        @pl.loop(0, span(reach) // UNROLL)
        def _(trip):
            for q in range(UNROLL):
                plane = begin + trip * UNROLL + q
                if head is not None:
                    head(plane + 1)
                if j0p < j0:
                    edges(plane, (j0p, j0))
                for low in range(rows_of(j0), rows_of(j1), CHUNK):
                    each(plane, low)

    def drive(window, reach_last):
        def amplitude(n, plane, at):
            return jnp.take_along_axis(
                table_ref[window * 9 + n], actor[plane, at, :], axis=1, mode="promise_in_bounds"
            )

        reach = reach_last + STEPS
        j0, j1 = columns(reach)

        @pl.loop(0, span(reach))
        def _(y):
            plane = lowest(reach) + y
            for low in range(rows_of(j0), rows_of(j1), CHUNK):
                at = pl.ds(low, CHUNK)
                push = (0.5 * mass[plane, at, :]) * amplitude(0, plane, at)
                for c in range(3):
                    disp[c, plane, at, :] = zero
                    vel[c, plane, at, :] = push * dirs[c, plane, at, :]

        for n in range(STEPS):
            reach = reach_last + STEPS - 1 - n
            j0, j1 = columns(reach + 1)
            last = n == STEPS - 1

            def head(plane):
                for low in range(rows_of(j0), rows_of(j1), CHUNK):
                    at = pl.ds(low, CHUNK)
                    for c in range(3):
                        disp[c, plane, at, :] = disp[c, plane, at, :] + vel[c, plane, at, :]

            def each(plane, low):
                at = pl.ds(low, CHUNK)
                centre, sums = parts(disp, div_u, plane, low)
                amp = amplitude(n + 1, plane, at)
                weight = mass[plane, at, :]
                for c in range(3):
                    six = six_x if c == 2 else 6.0
                    change = weight * ((dirs[c, plane, at, :] * amp + sums[c]) - six * centre[c])
                    if last:
                        vel[c, plane, at, :] = (vel[c, plane, at, :] + 0.5 * change) * (1.0 / time_step)
                    else:
                        vel[c, plane, at, :] = vel[c, plane, at, :] + change

            sweep(reach, [(disp, div_u)], head, each)

    def propagate(reach_last):
        even, odd = (disp, vel), (spare_u, spare_v)
        divs = (div_u, div_v)
        j0, j1 = columns(reach_last)
        begin = lowest(reach_last)

        def gather(k):
            @pl.loop(0, span(reach_last))
            def _(y):
                plane = begin + y
                for low in range(rows_of(j0), rows_of(j1), CHUNK):
                    at = pl.ds(low, CHUNK)
                    for c in range(3):
                        u0, v0 = (ref[c, plane, at, :] for ref in even)
                        u1, v1 = (ref[c, plane, at, :] for ref in odd)
                        new_u = (coef_c[k] * u0 + coef_s[k] * v0) + (
                            coef_c[k + 1] * u1 + coef_s[k + 1] * v1
                        )
                        new_v = (coef_c[k] * v0 - coef_g[k] * u0) + (
                            coef_c[k + 1] * v1 - coef_g[k + 1] * u1
                        )
                        if k:
                            new_u = total[c, plane, at, :] + new_u
                            new_v = total[3 + c, plane, at, :] + new_v
                        total[c, plane, at, :] = new_u
                        total[3 + c, plane, at, :] = new_v

        for k in range(1, TERMS):
            reach = reach_last + TERMS - 1 - k
            source, target = (even, odd) if k % 2 else (odd, even)

            def each(plane, low):
                at = pl.ds(low, CHUNK)
                weight = mass4[plane, at, :]
                middle = diag[plane, at, :]
                middle_x = diag_x[plane, at, :]
                for field, div, result in zip(source, divs, target):
                    centre, sums = parts(field, div, plane, low)
                    for c in range(3):
                        own_part = (middle_x if c == 2 else middle) * centre[c]
                        value = own_part - weight * sums[c]
                        if k == 1:
                            result[c, plane, at, :] = 0.5 * value
                        else:
                            result[c, plane, at, :] = value - result[c, plane, at, :]

            sweep(reach, list(zip(source, divs)), None, each)
            if k % 2:
                gather(k - 1)

    drive(0, 2 * (TERMS - 1))
    propagate(TERMS - 1)
    drive(1, TERMS - 1)
    j0, j1 = columns(TERMS - 1)

    @pl.loop(0, span(TERMS - 1))
    def _(y):
        plane = lowest(TERMS - 1) + y
        for low in range(rows_of(j0), rows_of(j1), CHUNK):
            at = pl.ds(low, CHUNK)
            for c in range(3):
                disp[c, plane, at, :] = disp[c, plane, at, :] + total[c, plane, at, :]
                vel[c, plane, at, :] = vel[c, plane, at, :] + total[3 + c, plane, at, :]

    propagate(0)
    drive(2, 0)

    @pl.loop(0, OWN_Y)
    def _(y):
        plane = home + 1 + y
        at = pl.ds(PAD + HALO, OWN_Z)
        for c in range(3):
            out_ref[c, y, :, :] = disp[c, plane, at, :] + total[c, plane, at, :]
            out_ref[3 + c, y, :, :] = vel[c, plane, at, :] + total[3 + c, plane, at, :]


def predict(place, table, far_left, left, own, right, far_right):
    box = (PLANES + 2, PAD + ROWS + PAD, LANES)
    f32 = jnp.float32
    vmem = pl.BlockSpec(memory_space=pltpu.VMEM)
    return pl.pallas_call(
        kernel,
        out_shape=jax.ShapeDtypeStruct((6, OWN_Y, OWN_Z, LANES), f32),
        in_specs=[pl.BlockSpec(memory_space=pltpu.SMEM)] + [vmem] * 6,
        out_specs=vmem,
        scratch_shapes=[pltpu.VMEM(box, f32)] * 4
        + [pltpu.VMEM(box, jnp.int32), pltpu.VMEM((3,) + box, f32)]
        + [pltpu.VMEM((3,) + box, f32)] * 4
        + [pltpu.VMEM((6,) + box, f32)]
        + [pltpu.VMEM(box, f32)] * 2,
        compiler_params=pltpu.CompilerParams(vmem_limit_bytes=60 * 1024 * 1024),
    )(place, table, far_left, left, own, right, far_right)


def lookup_tables(plan, profiles, directions):
    window = lax.axis_index("tm")
    count = lax.axis_size("tm")
    plans = [
        lax.ppermute(plan, "tm", [(i, i + back) for i in range(count - back)]) for back in (2, 1)
    ] + [plan]
    rows = []
    for back, ids in zip((2, 1, 0), plans):
        picked = ids[0][:, None] == jnp.arange(profiles.shape[0], dtype=jnp.int32)[None, :]
        picked = jnp.where(window >= back, picked, False).astype(jnp.float32)
        chosen = jnp.dot(
            picked, profiles, precision=lax.Precision.HIGHEST, preferred_element_type=jnp.float32
        )
        rows.append(chosen.T)
    table = jnp.concatenate(rows + [directions], axis=0)
    table = jnp.pad(table, ((0, 2), (0, LANES - table.shape[1])))
    return jnp.broadcast_to(table[:, None, :], (32, CHUNK, LANES))


def ring_steps(step):
    pairs = []
    for ring in range(8):
        move = step(ring)
        goal = (ring + move) % 8
        for y in range(4):
            source = ((ring // 4) * 4 + y) * 4 + ring % 4
            target = ((goal // 4) * 4 + y) * 4 + goal % 4
            pairs.append((source, target))
    return pairs


def body(inverse_mass, actuator_of_cell, plan_ids, profiles, directions):
    place = lax.axis_index("gy").astype(jnp.int32)[None]
    packed = jnp.stack([inverse_mass, actuator_of_cell.astype(jnp.float32)])
    table = lookup_tables(plan_ids, profiles, directions)
    from_lower = lax.ppermute(packed, ("tm", "gy"), ring_steps(lambda ring: 1))
    from_upper = lax.ppermute(packed, ("tm", "gy"), ring_steps(lambda ring: 7))
    opposite = lax.ppermute(packed, ("tm", "gy"), ring_steps(lambda ring: 2 if ring % 2 else 6))
    column = jnp.stack([packed, from_lower, opposite, from_upper])
    count = lax.axis_size("gz")

    def shifted(block, step):
        return lax.ppermute(
            block, "gz", [(i, i + step) for i in range(count) if 0 <= i + step < count]
        )

    left = shifted(column, 1)
    right = shifted(column, -1)
    far_left = shifted(column[..., 8:, :], 2)
    far_right = shifted(column[..., :8, :], -2)
    result = predict(place, table, far_left, left, column, right, far_right)
    return result[None]


def solution(mesh):
    in_specs = (P("gy", "gz", None), P("gy", "gz", None), P("tm", None), P(), P())
    out_specs = P("tm", None, "gy", "gz", None)
    return jax.shard_map(body, mesh=mesh, in_specs=in_specs, out_specs=out_specs, check_vma=False)
```

```python
import functools
import math

import jax
import jax.numpy as jnp
import numpy as np
from jax import lax
from jax.experimental import pallas as pl
from jax.experimental.pallas import tpu as pltpu
from jax.sharding import PartitionSpec as P

STEPS = 8
TERMS = 8
lame_ratio = 2.5
mass_top = 2.0
step_squared = 1.0

PLANES = 32
OWN_Y = 8
OWN_Z = 16
HALO = 24
ROWS = HALO + OWN_Z + HALO
PAD = 8
LANES = 128
CHUNK = 16
UNROLL = 4
BOX = PLANES + 2 * UNROLL + 4
NEAR = TERMS - 1


def cheb_tables():
    spectrum_top = mass_top * 12.0 * (1.0 + lame_ratio)
    time_step = math.sqrt(step_squared / spectrum_top)
    horizon = STEPS * time_step
    angles = np.pi * (np.arange(TERMS) + 0.5) / TERMS
    node_x = 0.5 * spectrum_top * (1.0 + np.cos(angles))
    node_root = np.sqrt(node_x)
    values_c = np.cos(horizon * node_root)
    values_s = np.sin(horizon * node_root) / node_root
    values_g = node_root * np.sin(horizon * node_root)

    def project_values(values):
        result = np.array([2.0 / TERMS * np.sum(values * np.cos(k * angles)) for k in range(TERMS)])
        result[0] = 0.5 * result[0]
        return [float(entry) for entry in result]

    return (
        spectrum_top,
        time_step,
        project_values(values_c),
        project_values(values_s),
        project_values(values_g),
    )


def columns(reach):
    return (HALO - reach) // 8, -(-(HALO + OWN_Z + reach) // 8)


def span(reach):
    count = min(8, reach) + OWN_Y + min(16, reach)
    return count + -count % UNROLL


def along_x():
    near = np.eye(LANES, k=1) + np.eye(LANES, k=-1) - 6.0 * np.eye(LANES)
    near_x = near.copy()
    near_x[0, 0] -= lame_ratio
    step = lame_ratio * (np.eye(LANES, k=-1) - np.eye(LANES))
    pair = np.concatenate([near_x, step], axis=1)
    near = np.concatenate([near, 0.0 * near], axis=1)
    return [jnp.asarray(np.concatenate([m, m]), jnp.bfloat16) for m in (near, pair)]


def lookup(table, index):
    numbers = lax.GatherDimensionNumbers(
        offset_dims=(), collapsed_slice_dims=(1,), start_index_map=(1,),
        operand_batching_dims=(0,), start_indices_batching_dims=(0,),
    )
    return lax.gather(
        table, index[..., None], numbers, (1, 1), mode=lax.GatherScatterMode.PROMISE_IN_BOUNDS
    )


def kernel(
    place_ref, near_ref, pair_ref, table_ref, far_left, left, own, right, far_right, out_ref,
    mass, mass4, actor, dirs, disp, vel, spare_u, spare_v, total, div_u, div_v,
):
    accs = [pltpu.ACC(0 if c < 2 else 1)((CHUNK, 2 * LANES), jnp.float32) for _ in range(2) for c in range(3) for _ in range(UNROLL) for _ in range(ROWS // CHUNK)]

    def scope(*held):
        pltpu.matmul_push_rhs(near_ref[...], 0, 0)
        pltpu.matmul_push_rhs(pair_ref[...], 0, 1)
        work(
            held, place_ref, table_ref, far_left, left, own, right, far_right, out_ref,
            mass, mass4, actor, dirs, disp, vel, spare_u, spare_v, total, div_u, div_v,
        )

    pl.run_scoped(scope, *accs)


def work(
    held, place_ref, table_ref, far_left, left, own, right, far_right, out_ref,
    mass, mass4, actor, dirs, disp, vel, spare_u, spare_v, total, div_u, div_v,
):
    spectrum_top, time_step, coef_c, coef_s, coef_g = cheb_tables()
    here = place_ref[0]
    home = here * OWN_Y
    fresh = [True, True]

    def acc_of(which, c, q, pair):
        return held[((which * 3 + c) * UNROLL + q) * (ROWS // CHUNK) + pair]

    def lane_of(value):
        return lax.broadcasted_iota(jnp.int32, value.shape, 1)

    def after(value):
        return jnp.where(lane_of(value) != LANES - 1, pltpu.roll(value, LANES - 1, 1), 0.0)

    def before(value):
        return jnp.where(lane_of(value) != 0, pltpu.roll(value, 1, 1), 0.0)

    def rows_of(column):
        return PAD + column * 8

    def lowest(reach):
        return jnp.clip(home - reach, 0, PLANES - span(reach)) + 1

    edge = jnp.zeros((PAD + ROWS + PAD, LANES), jnp.float32)
    for ref in (disp, vel, spare_u, spare_v):
        for c in range(3):
            for plane in [0] + list(range(PLANES + 1, BOX)):
                ref[c, plane, :, :] = edge

    for slot in range(4):
        first = lax.rem(here + 4 - slot, 4) * OWN_Y + 1

        @pl.loop(0, OWN_Y)
        def _(y):
            plane = first + y
            row = 0
            for piece in (far_left, left, own, right, far_right):
                for part in range(0, piece.shape[-2], 8):
                    at = pl.ds(PAD + row, 8)
                    weight = piece[slot, 0, y, part : part + 8, :] * (1.0 / spectrum_top)
                    index = piece[slot, 1, y, part : part + 8, :].astype(jnp.int32)
                    mass[plane, at, :] = weight
                    mass4[plane, at, :] = -4.0 * weight
                    actor[plane, at, :] = index
                    for c in range(3):
                        dirs[c, plane, at, :] = lookup(table_ref[27 + c, :8], index)
                    row += 8

    def divergence(field, plane, low):
        at = pl.ds(low, 8)
        u0, u1, u2 = (field[c, plane, at, :] for c in range(3))
        value = (field[0, plane + 1, at, :] - u0) + (field[1, plane, pl.ds(low + 1, 8), :] - u1)
        return (value + (after(u2) - u2)) * lame_ratio

    def spread(which, field, planes, cols):
        for pair, low in enumerate(range(rows_of(cols[0]), rows_of(cols[1]), CHUNK)):
            for q, plane in enumerate(planes):
                for c in range(3):
                    value = field[c, plane, pl.ds(low, CHUNK), :]
                    high = value.astype(jnp.bfloat16)
                    rest = (value - high.astype(jnp.float32)).astype(jnp.bfloat16)
                    unit = 0 if c < 2 else 1
                    pltpu.matmul_acc_lhs(
                        acc_of(which, c, q, pair),
                        jnp.concatenate([high, rest], axis=1),
                        load_staged_rhs=0 if fresh[unit] else None,
                    )
                    fresh[unit] = False

    def combine(which, field, div, planes, low, pair):
        at = pl.ds(low, CHUNK)
        around = [planes[0] - 1] + planes + [planes[-1] + 1]
        u = [[field[c, p, at, :] for p in around] for c in range(3)]
        p_before = div[around[0], at, :]
        found = []
        for q, plane in enumerate(planes):
            ahead = [field[c, plane, pl.ds(low + 1, CHUNK), :] for c in range(3)]
            behind = [field[c, plane, pl.ds(low - 1, CHUNK), :] for c in range(3)]
            centre = [u[c][q + 1] for c in range(3)]
            flat = [pltpu.matmul_pop(acc_of(which, c, q, pair)) for c in range(3)]
            step = flat[2][:, LANES:]
            p = ((u[0][q + 2] - centre[0]) + (ahead[1] - centre[1])) * lame_ratio + step
            div[plane, at, :] = p
            sums = [
                ((u[c][q] + u[c][q + 2]) + (ahead[c] + behind[c])) + (flat[c][:, :LANES] + p)
                for c in range(3)
            ]
            sums[0] = sums[0] - p_before
            sums[1] = sums[1] - div[plane, pl.ds(low - 1, CHUNK), :]
            sums[2] = sums[2] - before(p)
            p_before = p
            found.append((centre, sums))
        return found

    def sweep(reach, fields, head, each):
        j0, j1 = columns(reach)
        j0p = j0 - 1 if (HALO - reach) % 8 == 0 else j0
        begin = lowest(reach)

        def edges(plane, cols):
            for low in range(rows_of(cols[0]), rows_of(cols[1]), 8):
                for field, div in fields:
                    div[plane, pl.ds(low, 8), :] = divergence(field, plane, low)

        def prepare(first):
            for which, (field, div) in enumerate(fields):
                spread(which, field, [first + q for q in range(UNROLL)], (j0, j1))

        if head is not None:
            @pl.loop(0, 2 * UNROLL + 2)
            def _(i):
                head(begin - 1 + i)
        edges(begin - 1, (j0, j1))
        prepare(begin)

        @pl.loop(0, span(reach) // UNROLL)
        def _(trip):
            first = begin + trip * UNROLL
            planes = [first + q for q in range(UNROLL)]
            if j0p < j0:
                for plane in planes:
                    edges(plane, (j0p, j0))
            for pair, low in enumerate(range(rows_of(j0), rows_of(j1), CHUNK)):
                each(planes, low, pair)
            prepare(first + UNROLL)
            if head is not None:
                for q in range(UNROLL):
                    head(first + 2 * UNROLL + 1 + q)

        for which in range(len(fields)):
            for c in range(3):
                for q in range(UNROLL):
                    for pair in range((j1 - j0) // 2):
                        pltpu.matmul_pop(acc_of(which, c, q, pair))

    def drive(window, reach_last):
        def amplitude(n, plane, at):
            return lookup(table_ref[window * 9 + n], actor[plane, at, :])

        reach = reach_last + STEPS
        j0, j1 = columns(reach)

        @pl.loop(0, span(reach))
        def _(y):
            plane = lowest(reach) + y
            for low in range(rows_of(j0), rows_of(j1), CHUNK):
                at = pl.ds(low, CHUNK)
                push = (0.5 * mass[plane, at, :]) * amplitude(0, plane, at)
                for c in range(3):
                    moved = push * dirs[c, plane, at, :]
                    disp[c, plane, at, :] = moved
                    vel[c, plane, at, :] = moved

        for n in range(STEPS):
            reach = reach_last + STEPS - 1 - n
            j0, j1 = columns(reach + 1)
            last = n == STEPS - 1

            def head(plane):
                for low in range(rows_of(j0), rows_of(j1), CHUNK):
                    at = pl.ds(low, CHUNK)
                    for c in range(3):
                        disp[c, plane, at, :] = disp[c, plane, at, :] + vel[c, plane, at, :]

            def each(planes, low, pair):
                at = pl.ds(low, CHUNK)
                for plane, (centre, sums) in zip(planes, combine(0, disp, div_u, planes, low, pair)):
                    amp = amplitude(n + 1, plane, at)
                    weight = mass[plane, at, :]
                    for c in range(3):
                        change = weight * (dirs[c, plane, at, :] * amp + sums[c])
                        if last:
                            ended = vel[c, plane, at, :] + 0.5 * change
                            vel[c, plane, at, :] = ended * (1.0 / time_step)
                        else:
                            vel[c, plane, at, :] = vel[c, plane, at, :] + change

            sweep(reach, [(disp, div_u)], head if n else None, each)

    def propagate(reach_last):
        even, odd = (disp, vel), (spare_u, spare_v)
        divs = (div_u, div_v)
        j0, j1 = columns(reach_last)
        begin = lowest(reach_last)

        def gather(k):
            @pl.loop(0, span(reach_last))
            def _(y):
                plane = begin + y
                for low in range(rows_of(j0), rows_of(j1), CHUNK):
                    at = pl.ds(low, CHUNK)
                    to = pl.ds(low - rows_of(j0), CHUNK)
                    for c in range(3):
                        u0, v0 = (ref[c, plane, at, :] for ref in even)
                        u1, v1 = (ref[c, plane, at, :] for ref in odd)
                        new_u = (coef_c[k] * u0 + coef_s[k] * v0) + (
                            coef_c[k + 1] * u1 + coef_s[k + 1] * v1
                        )
                        new_v = (coef_c[k] * v0 - coef_g[k] * u0) + (
                            coef_c[k + 1] * v1 - coef_g[k + 1] * u1
                        )
                        if k:
                            new_u = total[c, y, to, :] + new_u
                            new_v = total[3 + c, y, to, :] + new_v
                        total[c, y, to, :] = new_u
                        total[3 + c, y, to, :] = new_v

        for k in range(1, TERMS):
            reach = reach_last + TERMS - 1 - k
            source, target = (even, odd) if k % 2 else (odd, even)

            def each(planes, low, pair):
                at = pl.ds(low, CHUNK)
                for which, (field, div, result) in enumerate(zip(source, divs, target)):
                    found = combine(which, field, div, planes, low, pair)
                    for plane, (centre, sums) in zip(planes, found):
                        weight = mass4[plane, at, :]
                        for c in range(3):
                            if k == 1:
                                value = (0.5 * weight) * sums[c] - centre[c]
                            else:
                                old = result[c, plane, at, :]
                                value = weight * sums[c] - ((centre[c] + centre[c]) + old)
                            result[c, plane, at, :] = value

            sweep(reach, list(zip(source, divs)), None, each)
            if k % 2:
                gather(k - 1)

    drive(0, 2 * (TERMS - 1))
    propagate(TERMS - 1)
    drive(1, TERMS - 1)
    j0, j1 = columns(TERMS - 1)

    @pl.loop(0, span(TERMS - 1))
    def _(y):
        plane = lowest(TERMS - 1) + y
        for low in range(rows_of(j0), rows_of(j1), CHUNK):
            at = pl.ds(low, CHUNK)
            to = pl.ds(low - rows_of(j0), CHUNK)
            for c in range(3):
                disp[c, plane, at, :] = disp[c, plane, at, :] + total[c, y, to, :]
                vel[c, plane, at, :] = vel[c, plane, at, :] + total[3 + c, y, to, :]

    propagate(0)
    drive(2, 0)

    @pl.loop(0, OWN_Y)
    def _(y):
        plane = home + 1 + y
        at = pl.ds(PAD + HALO, OWN_Z)
        for c in range(3):
            out_ref[c, y, :, :] = disp[c, plane, at, :] + total[c, y, :OWN_Z, :]
            out_ref[3 + c, y, :, :] = vel[c, plane, at, :] + total[3 + c, y, :OWN_Z, :]


def predict(place, table, far_left, left, own, right, far_right):
    box = (BOX, PAD + ROWS + PAD, LANES)
    f32 = jnp.float32
    vmem = pl.BlockSpec(memory_space=pltpu.VMEM)
    j0, j1 = columns(NEAR)
    return pl.pallas_call(
        kernel,
        out_shape=jax.ShapeDtypeStruct((6, OWN_Y, OWN_Z, LANES), f32),
        in_specs=[pl.BlockSpec(memory_space=pltpu.SMEM)] + [vmem] * 8,
        out_specs=vmem,
        scratch_shapes=[pltpu.VMEM(box, f32)] * 2
        + [pltpu.VMEM(box, jnp.int32), pltpu.VMEM((3,) + box, f32)]
        + [pltpu.VMEM((3,) + box, f32)] * 4
        + [pltpu.VMEM((6, span(NEAR), 8 * (j1 - j0), LANES), f32)]
        + [pltpu.VMEM(box, f32)] * 2,
        compiler_params=pltpu.CompilerParams(vmem_limit_bytes=60 * 1024 * 1024),
    )(place, *along_x(), table, far_left, left, own, right, far_right)


def lookup_tables(plan, profiles, directions):
    window = lax.axis_index("tm")
    count = lax.axis_size("tm")
    plans = [
        lax.ppermute(plan, "tm", [(i, i + back) for i in range(count - back)]) for back in (2, 1)
    ] + [plan]
    rows = []
    for back, ids in zip((2, 1, 0), plans):
        picked = ids[0][:, None] == jnp.arange(profiles.shape[0], dtype=jnp.int32)[None, :]
        picked = jnp.where(window >= back, picked, False).astype(jnp.float32)
        chosen = jnp.dot(
            picked, profiles, precision=lax.Precision.HIGHEST, preferred_element_type=jnp.float32
        )
        rows.append(chosen.T)
    table = jnp.concatenate(rows + [directions], axis=0)
    table = jnp.pad(table, ((0, 2), (0, LANES - table.shape[1])))
    return jnp.broadcast_to(table[:, None, :], (32, CHUNK, LANES))


def ring_steps(step):
    pairs = []
    for ring in range(8):
        move = step(ring)
        goal = (ring + move) % 8
        for y in range(4):
            source = ((ring // 4) * 4 + y) * 4 + ring % 4
            target = ((goal // 4) * 4 + y) * 4 + goal % 4
            pairs.append((source, target))
    return pairs


def body(inverse_mass, actuator_of_cell, plan_ids, profiles, directions):
    place = lax.axis_index("gy").astype(jnp.int32)[None]
    packed = jnp.stack([inverse_mass, actuator_of_cell.astype(jnp.float32)])
    table = lookup_tables(plan_ids, profiles, directions)
    from_lower = lax.ppermute(packed, ("tm", "gy"), ring_steps(lambda ring: 1))
    from_upper = lax.ppermute(packed, ("tm", "gy"), ring_steps(lambda ring: 7))
    opposite = lax.ppermute(packed, ("tm", "gy"), ring_steps(lambda ring: 2 if ring % 2 else 6))
    column = jnp.stack([packed, from_lower, opposite, from_upper])
    count = lax.axis_size("gz")

    def shifted(block, step):
        return lax.ppermute(
            block, "gz", [(i, i + step) for i in range(count) if 0 <= i + step < count]
        )

    left = shifted(column, 1)
    right = shifted(column, -1)
    far_left = shifted(column[..., 8:, :], 2)
    far_right = shifted(column[..., :8, :], -2)
    result = predict(place, table, far_left, left, column, right, far_right)
    return result[None]


def solution(mesh):
    in_specs = (P("gy", "gz", None), P("gy", "gz", None), P("tm", None), P(), P())
    out_specs = P("tm", None, "gy", "gz", None)
    return jax.shard_map(body, mesh=mesh, in_specs=in_specs, out_specs=out_specs, check_vma=False)
```
